256 devices in a mesh: pipe: 2 (over y_hi), tx: 16 (over y_lo, z), ty: 8 (over x, core).
Axes of the slice: x: 4, y: 4 (y_hi: 2, y_lo: 2; y = y_hi * 2 + y_lo), z: 8, core: 2. Of those that a mesh axis runs over, the one named last changes fastest.
Arguments:
- section_input: bfloat16 [2, 192, 8192], P('pipe', 'tx', 'ty'), may hold values from -6 to 6
- saved_input: bfloat16 [2, 192, 8192], P('pipe', 'tx', 'ty'), may hold values from -6 to 6
- out_grad: bfloat16 [2, 192, 8192], P('pipe', 'tx', 'ty'), may hold values from -6 to 6
- gate_weight: bfloat16 [2, 8192, 29568], P('pipe', 'ty', 'tx'), may hold values from -0.0625 to 0.0625
- up_weight: bfloat16 [2, 8192, 29568], P('pipe', 'ty', 'tx'), may hold values from -0.0625 to 0.0625
- down_weight: bfloat16 [2, 29568, 8192], P('pipe', 'tx', 'ty'), may hold values from -0.03125 to 0.03125
Outputs:
- next_input: bfloat16 [2, 192, 8192], P('pipe', 'tx', 'ty')
- prev_grad: bfloat16 [2, 192, 8192], P('pipe', 'tx', 'ty')
The draws below stay inside these ranges and needn't reach their ends.
All inputs are finite; a program needn't handle non-finite values.
Results may differ from the reference program's by a relative error of at most 0.0038.
Values may be sent and summed in bfloat16 or wider, within the bound.
A program may use at most 128 MiB of HBM per device.

```python
import jax
import jax.numpy as jnp
from jax import lax

D = 8192
FF = 29568
TOK = 192
SECTIONS = 2


def level_of(own_key, shape, pieces, smallest, top_value):
    loudness, own = 1.0, jax.random.fold_in(own_key, 6)
    for position, blocks in pieces:
        draws = jnp.exp(jax.random.uniform(jax.random.fold_in(own, position), (blocks,), jnp.float32, smallest / len(pieces), top_value / len(pieces)))
        loudness = loudness * jnp.repeat(draws, shape[position] // blocks).reshape([-1 if axis == position else 1 for axis in range(len(shape))])
    return loudness


def centred(rng, extent, width, bound, split=(), held_as=jnp.bfloat16):
    result = width * jax.random.normal(rng, extent, jnp.float32)
    if split:
        result = result * level_of(rng, extent, split, -0.22, 0.18)
    return jnp.clip(result, -bound, bound).astype(held_as)


def setup_inputs(seed: int = 0) -> dict:
    seeds = jax.random.split(jax.random.key(seed), 7)
    section_input = centred(seeds[0], (SECTIONS, TOK, D), 1.0, 6.0, ((0, 2), (1, 16), (2, 8)))
    saved_input = centred(seeds[1], (SECTIONS, TOK, D), 1.0, 6.0, ((0, 2), (1, 16), (2, 8)))
    out_grad = centred(seeds[2], (SECTIONS, TOK, D), 1.0, 6.0, ((0, 2), (1, 16), (2, 8)))
    gate_weight = centred(seeds[3], (SECTIONS, D, FF), D ** -0.5, 0.0625, ((0, 2), (1, 8), (2, 16)))
    up_weight = centred(seeds[4], (SECTIONS, D, FF), D ** -0.5, 0.0625, ((0, 2), (1, 8), (2, 16)))
    down_weight = centred(seeds[5], (SECTIONS, FF, D), FF ** -0.5, 0.03125, ((0, 2), (1, 16), (2, 8)))
    return dict(section_input=section_input, saved_input=saved_input, out_grad=out_grad, gate_weight=gate_weight, up_weight=up_weight, down_weight=down_weight)


def forward(inputs, wgate, wup, wdown):
    gate = jnp.dot(inputs, wgate, preferred_element_type=jnp.float32)
    up = jnp.dot(inputs, wup, preferred_element_type=jnp.float32)
    hidden = (jax.nn.silu(gate) * up).astype(jnp.bfloat16)
    mixed = jnp.dot(hidden, wdown, preferred_element_type=jnp.float32)
    return (inputs.astype(jnp.float32) + mixed).astype(jnp.bfloat16)


def backward(saved, grads, wgate, wup, wdown):
    dims = (((1,), (1,)), ((), ()))
    gate = jnp.dot(saved, wgate, preferred_element_type=jnp.float32)
    up = jnp.dot(saved, wup, preferred_element_type=jnp.float32)
    hidden_grad = lax.dot_general(grads, wdown, dims, preferred_element_type=jnp.float32)
    sigma = jax.nn.sigmoid(gate)
    gate_grad = (hidden_grad * up * sigma * (1.0 + gate * (1.0 - sigma))).astype(jnp.bfloat16)
    up_grad = (hidden_grad * gate * sigma).astype(jnp.bfloat16)
    total = grads.astype(jnp.float32)
    total = total + lax.dot_general(gate_grad, wgate, dims, preferred_element_type=jnp.float32)
    total = total + lax.dot_general(up_grad, wup, dims, preferred_element_type=jnp.float32)
    return total.astype(jnp.bfloat16)


def reference(section_input, saved_input, out_grad, gate_weight, up_weight, down_weight):
    outputs = []
    gradients = []
    for section in range(SECTIONS):
        outputs.append(forward(section_input[section], gate_weight[section], up_weight[section], down_weight[section]))
        gradients.append(backward(saved_input[section], out_grad[section], gate_weight[section], up_weight[section], down_weight[section]))
    next_input = jnp.roll(jnp.stack(outputs), 1, axis=0)
    prev_grad = jnp.roll(jnp.stack(gradients), -1, axis=0)
    return next_input, prev_grad
```

```python
import jax
import jax.numpy as jnp
from jax import lax
from jax.experimental import pallas as pl
from jax.experimental.pallas import tpu as pltpu
from jax.sharding import PartitionSpec as P

MESH = pl.DeviceIdType.MESH
F32 = jnp.float32
BF16 = jnp.bfloat16
CONTRACT_LAST = (((1,), (1,)), ((), ()))
N_SEM = 192


def chunks_of(total):
    widths = [256, 256, 320, 256, 256, 256]
    widths.append(total - sum(widths))
    starts = [sum(widths[:i]) for i in range(len(widths))]
    return list(zip(starts, widths))


def kernel(chunks, si, sv, og, wg_hbm, wu_hbm, wd_hbm, both_out, *scratch):
    (wg, wu, wd, tmp, packs, xf, xb, acc_m, acc_b, pkf, ys, yr,
     z4s, z4r, zs, zr, fin, fin_r, wsem, ssem, rsem) = scratch[:21]
    per_chunk = [scratch[21 + 9 * c: 30 + 9 * c] for c in range(len(chunks))]

    pipe = lax.axis_index("pipe")
    tx = lax.axis_index("tx")
    ty = lax.axis_index("ty")
    ylo, z = tx // 8, tx % 8
    x, core = ty // 2, ty % 2
    partner = {"ty": x * 2 + (1 - core)}
    xp = {"ty": ((x + 1) % 4) * 2 + core}
    xm = {"ty": ((x + 3) % 4) * 2 + core}
    yp = {"tx": (1 - ylo) * 8 + z}
    zp = {"tx": ylo * 8 + (z + 1) % 8}
    zm = {"tx": ylo * 8 + (z + 7) % 8}
    along_z = {k: {"tx": ylo * 8 + (z + k) % 8} for k in (2, 3, 5, 6)}
    along_z[1], along_z[7] = zp, zm
    across = {"pipe": 1 - pipe, "tx": (1 - ylo) * 8 + z}

    loads = [
        pltpu.make_async_copy(wg_hbm.at[0], wg, wsem.at[0]),
        pltpu.make_async_copy(wu_hbm.at[0], wu, wsem.at[1]),
        pltpu.make_async_copy(wd_hbm.at[0], wd, wsem.at[2]),
    ]
    for load in loads:
        load.start()

    tmp[0:12] = si[...].astype(F32)
    tmp[12:24] = og[...].astype(F32)
    tmp[24:36] = sv[...].astype(F32)
    packs[0, 0] = tmp[...].astype(BF16)

    barrier = pltpu.get_barrier_semaphore()
    neighbours = (partner, xp, xm, yp, across) + tuple(along_z.values())
    for neighbour in neighbours:
        pl.semaphore_signal(barrier, inc=1, device_id=neighbour, device_id_type=MESH)
    pl.semaphore_wait(barrier, len(neighbours))

    sent = []

    def send(src, dst, device):
        k = len(sent)
        copy = pltpu.make_async_remote_copy(
            src_ref=src, dst_ref=dst, send_sem=ssem.at[k], recv_sem=rsem.at[k],
            device_id=device, device_id_type=MESH,
        )
        copy.start()
        sent.append(copy)
        return copy

    def pos_of(j):
        owner, own_core = j // 2, j % 2
        r = (owner - x + 4) % 4
        rc = jnp.where(core == own_core, 0, 1)
        return rc * 4 + r

    def place(yrel, zrel):
        pos = pos_of(yrel * 4 + zrel // 2)
        lo = 12 * (zrel % 2)
        piece = packs[yrel, zrel].astype(F32)
        xf[0, pos, lo:lo + 12] = piece[0:12]
        xf[1, pos, lo:lo + 12] = piece[24:36]
        xf[2, pos, lo:lo + 12] = piece[12:24]

    lanes = packs.shape[-1] // 2

    def hop(source, target, device, before=None):
        copies = []
        for part in range(2):
            if before is not None:
                before[part].wait_recv()
            cols = slice(lanes * part, lanes * part + lanes)
            copies.append(send(packs.at[source[0], source[1], :, cols],
                               packs.at[target[0], target[1], :, cols], device))
        return copies

    def arrived(copies):
        for copy in copies:
            copy.wait_recv()

    y0, p1, m1 = [], [], []
    for part in range(2):
        cols = slice(lanes * part, lanes * part + lanes)
        mine = packs.at[0, 0, :, cols]
        p1.append(send(mine, packs.at[0, 7, :, cols], zp))
        m1.append(send(mine, packs.at[0, 1, :, cols], zm))
        y0.append(send(mine, packs.at[1, 0, :, cols], yp))
    place(0, 0)
    p2 = hop((0, 7), (0, 6), zp, p1)
    m2 = hop((0, 1), (0, 2), zm, m1)
    arrived(y0)
    q1 = hop((1, 0), (1, 7), zp)
    n1 = hop((1, 0), (1, 1), zm)
    place(1, 0)
    place(0, 7)
    place(0, 1)
    p3 = hop((0, 6), (0, 5), zp, p2)
    y6 = hop((0, 6), (1, 6), yp)
    m3 = hop((0, 2), (0, 3), zm, m2)
    place(0, 6)
    place(0, 2)
    n2 = hop((1, 1), (1, 2), zm, n1)
    place(1, 1)
    p4 = hop((0, 5), (0, 4), zp, p3)
    y5 = hop((0, 5), (1, 5), yp)
    y3 = hop((0, 3), (1, 3), yp, m3)
    place(0, 5)
    place(0, 3)
    arrived(q1)
    place(1, 7)
    arrived(y6)
    place(1, 6)
    y4 = hop((0, 4), (1, 4), yp, p4)
    place(0, 4)
    arrived(n2)
    place(1, 2)
    arrived(y5)
    place(1, 5)
    arrived(y3)
    place(1, 3)
    arrived(y4)
    place(1, 4)

    for a in range(3):
        xb[192 * a:192 * a + 192] = xf[a].reshape(192, xf.shape[-1]).astype(BF16)
    for load in loads:
        load.wait()

    state = [dict() for _ in chunks]

    def compute(c):
        lo, n = chunks[c]
        own, sp, rp = per_chunk[c][:3]

        def keep(values, array):
            for r in range(4):
                own[r, array] = values[24 * r:24 * r + 24]
                sp[r, array] = values[96 + 24 * r:120 + 24 * r]

        for first, weight in ((0, wg), (1, wu)):
            both = lax.dot_general(xb[0:384], weight[lo:lo + n, :], CONTRACT_LAST,
                                   preferred_element_type=F32)
            keep(both[0:192], first)
            keep(both[192:384], first + 2)
        keep(lax.dot_general(xb[384:576], wd[lo:lo + n, :], CONTRACT_LAST,
                             preferred_element_type=F32), 4)
        state[c]["pair"] = send(sp.at[2:4], rp.at[2:4], partner)
        state[c]["pair2"] = send(sp.at[0:2], rp.at[0:2], partner)

    def stage_a(c):
        own, sp, rp, m1s, m1r = per_chunk[c][:5]
        na = 3 if c % 2 == 0 else 2
        state[c]["pair"].wait_recv()
        m1s[...] = (own[2] + rp[2]).astype(BF16)
        state[c]["m1p"] = send(m1s.at[0:na], m1r.at[0:na], xp)
        state[c]["m1m"] = send(m1s.at[na:5], m1r.at[na:5], xm)

    def stage_b(c):
        own, sp, rp, m1s, m1r, m2s, m2r = per_chunk[c][:7]
        na = 3 if c % 2 == 0 else 2
        state[c]["pair2"].wait_recv()
        state[c]["m1p"].wait_recv()
        for a in range(5):
            total = own[1, a] + rp[1, a]
            if a < na:
                total = total + m1r[a].astype(F32)
            m2s[0, a] = total.astype(BF16)
        state[c]["m2p"] = send(m2s.at[0], m2r.at[0], xp)
        state[c]["m1m"].wait_recv()
        for a in range(5):
            total = own[3, a] + rp[3, a]
            if a >= na:
                total = total + m1r[a].astype(F32)
            m2s[1, a] = total.astype(BF16)
        state[c]["m2m"] = send(m2s.at[1], m2r.at[1], xm)

    def stage_c(c):
        own, sp, rp, m1s, m1r, m2s, m2r, h = per_chunk[c][:8]
        state[c]["m2p"].wait_recv()
        state[c]["m2m"].wait_recv()
        gate, up, sgate, sup, hgrad = [
            own[0, a] + rp[0, a] + m2r[0, a].astype(F32) + m2r[1, a].astype(F32)
            for a in range(5)
        ]
        h[0, 0] = (gate * jax.nn.sigmoid(gate) * up).astype(BF16)
        q = jax.nn.sigmoid(sgate)
        h[1, 0] = (hgrad * sup * q * (1.0 + sgate * (1.0 - q))).astype(BF16)
        h[2, 0] = (hgrad * sgate * q).astype(BF16)
        state[c]["hp"] = send(h.at[:, 0], h.at[:, 3], xp)
        state[c]["hm"] = send(h.at[:, 0], h.at[:, 1], xm)
        state[c]["h0"] = send(h.at[:, 0], h.at[:, 4], partner)

    def stage_d(c):
        h = per_chunk[c][7]
        nb = 1 if c % 2 == 0 else 2
        state[c]["hp"].wait_recv()
        state[c]["hpp"] = send(h.at[0:nb, 3], h.at[0:nb, 2], xp)
        state[c]["hm"].wait_recv()
        state[c]["hmm"] = send(h.at[nb:3, 1], h.at[nb:3, 2], xm)
        state[c]["h3"] = send(h.at[:, 3], h.at[:, 7], partner)
        state[c]["h1"] = send(h.at[:, 1], h.at[:, 5], partner)

    def stage_e(c):
        h = per_chunk[c][7]
        state[c]["hpp"].wait_recv()
        state[c]["hmm"].wait_recv()
        state[c]["h2"] = send(h.at[:, 2], h.at[:, 6], partner)

    def stage_f(c):
        lo, n = chunks[c]
        h = per_chunk[c][7]
        for name in ("h0", "h1", "h3", "h2"):
            state[c][name].wait_recv()
        hidden, ggrad, ugrad = [
            h[a].astype(F32).reshape(192, n).astype(BF16) for a in range(3)
        ]
        mixed = jnp.dot(hidden, wd[lo:lo + n, :], preferred_element_type=F32)
        back = jnp.dot(ggrad, wg[lo:lo + n, :], preferred_element_type=F32)
        back = back + jnp.dot(ugrad, wu[lo:lo + n, :], preferred_element_type=F32)
        mixed = mixed.reshape(8, 24, 1024)
        back = back.reshape(8, 24, 1024)
        if c > 0:
            mixed = mixed + acc_m[...]
            back = back + acc_b[...]
        acc_m[...] = mixed
        acc_b[...] = back

    stages = (compute, stage_a, stage_b, stage_c, stage_d, stage_e, stage_f)
    count = len(chunks)
    for step in range(count + len(stages) - 1):
        for depth, stage in enumerate(stages):
            c = step - depth
            if 0 <= c < count:
                stage(c)

    order = (4, 2, 6, 3, 5, 1, 7, 0)
    ycopies = {}
    for yrel in (0, 1):
        for k in order:
            pos = pos_of(yrel * 4 + k // 2)
            lo = 12 * (k % 2)
            pkf[yrel, k, 0:12] = acc_m[pos, lo:lo + 12]
            pkf[yrel, k, 12:24] = acc_b[pos, lo:lo + 12]
            if yrel == 0:
                ys[k] = pkf[0, k].astype(BF16)
                ycopies[k] = send(ys.at[k], yr.at[k], yp)

    def summed(k):
        ycopies[k].wait_recv()
        return pkf[1, k] + yr[k].astype(F32)

    four = summed(4)
    z4s[0] = four[:, 0:512].astype(BF16)
    z4s[1] = four[:, 512:1024].astype(BF16)
    relays = {3: send(z4s.at[0], z4r.at[0], zp), 5: send(z4s.at[1], z4r.at[1], zm)}
    zcopies = {}
    for k in order[1:7]:
        fresh = summed(k)
        if k in relays:
            way = 0 if k == 3 else 1
            relays[k].wait_recv()
            cols = slice(512 * way, 512 * way + 512)
            other = slice(512 - 512 * way, 1024 - 512 * way)
            zs[k, :, cols] = (fresh[:, cols] + z4r[way].astype(F32)).astype(BF16)
            zs[k, :, other] = fresh[:, other].astype(BF16)
        else:
            zs[k] = fresh.astype(BF16)
        zcopies[k] = send(zs.at[k], zr.at[k], along_z[k])
    total = summed(0) + packs[1, 0].astype(F32)[0:24]
    for k in order[1:7]:
        zcopies[k].wait_recv()
        total = total + zr[k].astype(F32)
    fin[...] = total.astype(BF16)
    last = send(fin, fin_r, across)
    last.wait_recv()
    both_out[...] = fin_r[...]
    for copy in sent:
        copy.wait_send()


def local(section_input, saved_input, out_grad, gate_weight, up_weight, down_weight):
    width, hidden = gate_weight.shape[1:]
    chunks = chunks_of(hidden)
    vmem = pltpu.VMEM
    scratch = [
        vmem((hidden, width), BF16),
        vmem((hidden, width), BF16),
        vmem((hidden, width), BF16),
        vmem((36, width), F32),
        vmem((2, 8, 36, width), BF16),
        vmem((3, 8, 24, width), F32),
        vmem((576, width), BF16),
        vmem((8, 24, width), F32),
        vmem((8, 24, width), F32),
        vmem((2, 8, 24, width), F32),
        vmem((8, 24, width), BF16),
        vmem((8, 24, width), BF16),
        vmem((2, 24, 512), BF16),
        vmem((2, 24, 512), BF16),
        vmem((8, 24, width), BF16),
        vmem((8, 24, width), BF16),
        vmem((24, width), BF16),
        vmem((24, width), BF16),
        pltpu.SemaphoreType.DMA((3,)),
        pltpu.SemaphoreType.DMA((N_SEM,)),
        pltpu.SemaphoreType.DMA((N_SEM,)),
    ]
    for _, n in chunks:
        scratch += [
            vmem((4, 5, 24, n), F32),
            vmem((4, 5, 24, n), F32),
            vmem((4, 5, 24, n), F32),
            vmem((5, 24, n), BF16),
            vmem((5, 24, n), BF16),
            vmem((2, 5, 24, n), BF16),
            vmem((2, 5, 24, n), BF16),
            vmem((3, 8, 24, n), BF16),
            vmem((8, 128), F32),
        ]

    def body(*refs):
        kernel(chunks, *refs)

    inside = pl.BlockSpec(memory_space=pltpu.VMEM)
    outside = pl.BlockSpec(memory_space=pl.ANY)
    both = pl.pallas_call(
        body,
        out_shape=jax.ShapeDtypeStruct((24, width), BF16),
        in_specs=[inside] * 3 + [outside] * 3,
        out_specs=inside,
        scratch_shapes=scratch,
        compiler_params=pltpu.CompilerParams(
            collective_id=0, has_side_effects=True, vmem_limit_bytes=60 * 1024 * 1024
        ),
    )(section_input[0], saved_input[0], out_grad[0], gate_weight.swapaxes(1, 2),
      up_weight.swapaxes(1, 2), down_weight)
    return both[None, 0:12], both[None, 12:24]


def solution(mesh):
    spread = P("pipe", "tx", "ty")
    return jax.shard_map(
        local,
        mesh=mesh,
        in_specs=(spread, spread, spread, P("pipe", "ty", "tx"), P("pipe", "ty", "tx"), spread),
        out_specs=(spread, spread),
        check_vma=False,
    )
```

```python
import jax
import jax.numpy as jnp
from jax import lax
from jax.experimental import pallas as pl
from jax.experimental.pallas import tpu as pltpu
from jax.sharding import PartitionSpec as P

MESH = pl.DeviceIdType.MESH
F32 = jnp.float32
BF16 = jnp.bfloat16
CONTRACT_LAST = (((1,), (1,)), ((), ()))
N_SEM = 192


def plan_of(total):
    own = -(-total // 32) * 16
    widths = [256] * (own // 256)
    widths.append(own - sum(widths))
    items = [(half, sum(widths[:i]), w) for half in range(2) for i, w in enumerate(widths)]
    return own, items


def kernel(own_units, items, si, sv, og, wg_hbm, wu_hbm, wd_hbm, both_out, *scratch):
    (wg, wu, wd, tmp, packs, xf, xb, acc_m, acc_b, pkf, ys, yr,
     z4s, z4r, zs, zr, fin, fin_r, wsem, ssem, rsem) = scratch[:21]
    per_chunk = [scratch[21 + 8 * c: 29 + 8 * c] for c in range(len(items))]

    pipe = lax.axis_index("pipe")
    tx = lax.axis_index("tx")
    ty = lax.axis_index("ty")
    ylo, z = tx // 8, tx % 8
    x, core = ty // 2, ty % 2
    partner = {"ty": x * 2 + (1 - core)}
    xp = {"ty": ((x + 1) % 4) * 2 + core}
    xm = {"ty": ((x + 3) % 4) * 2 + core}
    yp = {"tx": (1 - ylo) * 8 + z}
    zp = {"tx": ylo * 8 + (z + 1) % 8}
    zm = {"tx": ylo * 8 + (z + 7) % 8}
    across = {"pipe": 1 - pipe, "tx": (1 - ylo) * 8 + z}

    units = wd_hbm.shape[1]
    loads = [
        pltpu.make_async_copy(wg_hbm.at[0], wg.at[0:units], wsem.at[0]),
        pltpu.make_async_copy(wu_hbm.at[0], wu.at[0:units], wsem.at[1]),
        pltpu.make_async_copy(wd_hbm.at[0], wd.at[0:units], wsem.at[2]),
    ]
    for load in loads:
        load.start()
    for weight in (wg, wu, wd):
        weight[units:2 * own_units] = jnp.zeros((2 * own_units - units, weight.shape[1]), BF16)

    tmp[0:12] = si[...].astype(F32)
    tmp[12:24] = og[...].astype(F32)
    tmp[24:36] = sv[...].astype(F32)
    packs[0, 0] = tmp[...].astype(BF16)

    barrier = pltpu.get_barrier_semaphore()
    neighbours = (partner, xp, xm, yp, zp, zm, across)
    for neighbour in neighbours:
        pl.semaphore_signal(barrier, inc=1, device_id=neighbour, device_id_type=MESH)
    pl.semaphore_wait(barrier, len(neighbours))

    sent = []

    def send(src, dst, device):
        k = len(sent)
        copy = pltpu.make_async_remote_copy(
            src_ref=src, dst_ref=dst, send_sem=ssem.at[k], recv_sem=rsem.at[k],
            device_id=device, device_id_type=MESH,
        )
        copy.start()
        sent.append(copy)
        return copy

    def slab_of(zrel):
        return (zrel // 2 - x + 4) % 4

    def place(yrel, zrel):
        r = slab_of(zrel)
        lo = 12 * (zrel % 2)
        piece = packs[yrel, zrel].astype(F32)
        xf[0, yrel, r, lo:lo + 12] = piece[0:12]
        xf[1, yrel, r, lo:lo + 12] = piece[24:36]
        xf[2, yrel, r, lo:lo + 12] = piece[12:24]

    def operands(half):
        for a in range(3):
            xb[half, 96 * a:96 * a + 96] = xf[a, half].reshape(96, xf.shape[-1]).astype(BF16)

    lanes = packs.shape[-1] // 2

    def hop(source, target, device, before=None):
        copies = []
        for part in range(2):
            if before is not None:
                before[part].wait_recv()
            cols = slice(lanes * part, lanes * part + lanes)
            copies.append(send(packs.at[source[0], source[1], :, cols],
                               packs.at[target[0], target[1], :, cols], device))
        return copies

    def arrived(copies):
        for copy in copies:
            copy.wait_recv()

    y0, p1, m1 = [], [], []
    for part in range(2):
        cols = slice(lanes * part, lanes * part + lanes)
        mine = packs.at[0, 0, :, cols]
        p1.append(send(mine, packs.at[0, 7, :, cols], zp))
        m1.append(send(mine, packs.at[0, 1, :, cols], zm))
        y0.append(send(mine, packs.at[1, 0, :, cols], yp))
    place(0, 0)
    p2 = hop((0, 7), (0, 6), zp, p1)
    m2 = hop((0, 1), (0, 2), zm, m1)
    y7 = hop((0, 7), (1, 7), yp)
    y1 = hop((0, 1), (1, 1), yp)
    place(0, 7)
    place(0, 1)
    p3 = hop((0, 6), (0, 5), zp, p2)
    m3 = hop((0, 2), (0, 3), zm, m2)
    y6 = hop((0, 6), (1, 6), yp)
    y2 = hop((0, 2), (1, 2), yp)
    place(0, 6)
    place(0, 2)
    p4 = hop((0, 5), (0, 4), zp, p3)
    y5 = hop((0, 5), (1, 5), yp)
    y3 = hop((0, 3), (1, 3), yp, m3)
    place(0, 5)
    place(0, 3)
    y4 = hop((0, 4), (1, 4), yp, p4)
    place(0, 4)
    operands(0)
    for load in loads:
        load.wait()

    def second_half():
        for k, copies in ((0, y0), (7, y7), (1, y1), (6, y6), (2, y2), (5, y5), (3, y3), (4, y4)):
            arrived(copies)
            place(1, k)
        operands(1)

    state = [dict() for _ in items]

    def rows_of(c):
        half, offset, n = items[c]
        return [pl.ds(pl.multiple_of(who * own_units + offset, 16), n)
                for who in (core, 1 - core)]

    def compute(c):
        half, offset, n = items[c]
        own, sp, rp = per_chunk[c][:3]
        for target, rows in zip((own, sp), rows_of(c)):
            def keep(values, array):
                for r in range(4):
                    target[r, array] = values[24 * r:24 * r + 24]

            for first, weight in ((0, wg), (1, wu)):
                both = lax.dot_general(xb[half, 0:192], weight[rows, :], CONTRACT_LAST,
                                       preferred_element_type=F32)
                keep(both[0:96], first)
                keep(both[96:192], first + 2)
            keep(lax.dot_general(xb[half, 192:288], wd[rows, :], CONTRACT_LAST,
                                 preferred_element_type=F32), 4)
        state[c]["pair"] = send(sp.at[2:4], rp.at[2:4], partner)
        state[c]["pair2"] = send(sp.at[0:2], rp.at[0:2], partner)

    def stage_a(c):
        own, sp, rp, m1s, m1r = per_chunk[c][:5]
        na = 3 if c % 2 == 0 else 2
        state[c]["pair"].wait_recv()
        m1s[...] = (own[2] + rp[2]).astype(BF16)
        state[c]["m1p"] = send(m1s.at[0:na], m1r.at[0:na], xp)
        state[c]["m1m"] = send(m1s.at[na:5], m1r.at[na:5], xm)

    def stage_b(c):
        own, sp, rp, m1s, m1r, m2s, m2r = per_chunk[c][:7]
        na = 3 if c % 2 == 0 else 2
        state[c]["pair2"].wait_recv()
        state[c]["m1p"].wait_recv()
        for a in range(5):
            total = own[1, a] + rp[1, a]
            if a < na:
                total = total + m1r[a].astype(F32)
            m2s[0, a] = total.astype(BF16)
        state[c]["m2p"] = send(m2s.at[0], m2r.at[0], xp)
        state[c]["m1m"].wait_recv()
        for a in range(5):
            total = own[3, a] + rp[3, a]
            if a >= na:
                total = total + m1r[a].astype(F32)
            m2s[1, a] = total.astype(BF16)
        state[c]["m2m"] = send(m2s.at[1], m2r.at[1], xm)

    def stage_c(c):
        own, sp, rp, m1s, m1r, m2s, m2r, h = per_chunk[c][:8]
        state[c]["m2p"].wait_recv()
        state[c]["m2m"].wait_recv()
        gate, up, sgate, sup, hgrad = [
            own[0, a] + rp[0, a] + m2r[0, a].astype(F32) + m2r[1, a].astype(F32)
            for a in range(5)
        ]
        h[0, 0] = (gate * jax.nn.sigmoid(gate) * up).astype(BF16)
        q = jax.nn.sigmoid(sgate)
        h[1, 0] = (hgrad * sup * q * (1.0 + sgate * (1.0 - q))).astype(BF16)
        h[2, 0] = (hgrad * sgate * q).astype(BF16)
        state[c]["hp"] = send(h.at[:, 0], h.at[:, 3], xp)
        state[c]["hm"] = send(h.at[:, 0], h.at[:, 1], xm)
        state[c]["h0"] = send(h.at[:, 0], h.at[:, 4], partner)

    def stage_d(c):
        h = per_chunk[c][7]
        nb = 1 if c % 2 == 0 else 2
        state[c]["hp"].wait_recv()
        state[c]["hpp"] = send(h.at[0:nb, 3], h.at[0:nb, 2], xp)
        state[c]["hm"].wait_recv()
        state[c]["hmm"] = send(h.at[nb:3, 1], h.at[nb:3, 2], xm)
        state[c]["h3"] = send(h.at[:, 3], h.at[:, 7], partner)
        state[c]["h1"] = send(h.at[:, 1], h.at[:, 5], partner)

    def stage_e(c):
        h = per_chunk[c][7]
        state[c]["hpp"].wait_recv()
        state[c]["hmm"].wait_recv()
        state[c]["h2"] = send(h.at[:, 2], h.at[:, 6], partner)

    def stage_f(c):
        half, offset, n = items[c]
        h = per_chunk[c][7]
        for name in ("h0", "h1", "h3", "h2"):
            state[c][name].wait_recv()
        mixed, back = None, None
        for part, rows in enumerate(rows_of(c)):
            hidden, ggrad, ugrad = [
                h[a, 4 * part:4 * part + 4].astype(F32).reshape(96, n).astype(BF16)
                for a in range(3)
            ]
            one = jnp.dot(hidden, wd[rows, :], preferred_element_type=F32)
            two = jnp.dot(ggrad, wg[rows, :], preferred_element_type=F32)
            two = two + jnp.dot(ugrad, wu[rows, :], preferred_element_type=F32)
            mixed = one if mixed is None else mixed + one
            back = two if back is None else back + two
        mixed = mixed.reshape(4, 24, 1024)
        back = back.reshape(4, 24, 1024)
        if offset > 0:
            mixed = mixed + acc_m[half]
            back = back + acc_b[half]
        acc_m[half] = mixed
        acc_b[half] = back

    def packet(half, k):
        r = slab_of(k)
        lo = 12 * (k % 2)
        pkf[half, k, 0:12] = acc_m[half, r, lo:lo + 12]
        pkf[half, k, 12:24] = acc_b[half, r, lo:lo + 12]
        return pkf[half, k]

    ycopies = {}

    def first_sums():
        for k in (4, 3, 5, 2, 6, 1, 7, 0):
            ys[k] = packet(0, k).astype(BF16)
            ycopies[k] = send(ys.at[k], yr.at[k], yp)

    stages = (compute, stage_a, stage_b, stage_c, stage_d, stage_e, stage_f)
    count = len(items)
    for step in range(count + len(stages) - 1):
        if step == count // 2:
            second_half()
        for depth, stage in enumerate(stages):
            c = step - depth
            if 0 <= c < count:
                stage(c)
                if stage is stage_f and c == count // 2 - 1:
                    first_sums()

    def summed(k):
        ycopies[k].wait_recv()
        return packet(1, k) + yr[k].astype(F32)

    def cols_of(part):
        return slice(512 * part, 512 * part + 512)

    four = summed(4)
    links = ((0, zp, -1), (1, zm, 1))
    chain = {}
    for way, device, sign in links:
        z4s[way] = four[:, cols_of(way)].astype(BF16)
        chain[way, way] = send(z4s.at[way], z4r.at[way], device)
    for step in range(3):
        fresh = [summed(4 + sign * (step + 1)) for way, device, sign in links]
        for turn in range(2):
            for way, device, sign in links:
                part = 1 - way if turn == 0 else way
                cols = cols_of(part)
                value = fresh[way][:, cols]
                if step > 0 or part == way:
                    chain[way, part].wait_recv()
                    value = value + (z4r[way] if step == 0 else zr[way, step - 1, :, cols]).astype(F32)
                zs[way, step, :, cols] = value.astype(BF16)
                chain[way, part] = send(zs.at[way, step, :, cols], zr.at[way, step, :, cols], device)
    total = summed(0) + packs[1, 0].astype(F32)[0:24]
    last = []
    for part in range(2):
        cols = cols_of(part)
        value = total[:, cols]
        for way in range(2):
            chain[way, part].wait_recv()
            value = value + zr[way, 2, :, cols].astype(F32)
        fin[:, cols] = value.astype(BF16)
        last.append(send(fin.at[:, cols], fin_r.at[:, cols], across))
    arrived(last)
    both_out[...] = fin_r[...]
    for copy in sent:
        copy.wait_send()


def local(section_input, saved_input, out_grad, gate_weight, up_weight, down_weight):
    width, hidden = gate_weight.shape[1:]
    own, items = plan_of(hidden)
    rows = 2 * own
    vmem = pltpu.VMEM
    scratch = [
        vmem((rows, width), BF16),
        vmem((rows, width), BF16),
        vmem((rows, width), BF16),
        vmem((36, width), F32),
        vmem((2, 8, 36, width), BF16),
        vmem((3, 2, 4, 24, width), F32),
        vmem((2, 288, width), BF16),
        vmem((2, 4, 24, width), F32),
        vmem((2, 4, 24, width), F32),
        vmem((2, 8, 24, width), F32),
        vmem((8, 24, width), BF16),
        vmem((8, 24, width), BF16),
        vmem((2, 24, 512), BF16),
        vmem((2, 24, 512), BF16),
        vmem((2, 3, 24, width), BF16),
        vmem((2, 3, 24, width), BF16),
        vmem((24, width), BF16),
        vmem((24, width), BF16),
        pltpu.SemaphoreType.DMA((3,)),
        pltpu.SemaphoreType.DMA((N_SEM,)),
        pltpu.SemaphoreType.DMA((N_SEM,)),
    ]
    for _, _, n in items:
        scratch += [
            vmem((4, 5, 24, n), F32),
            vmem((4, 5, 24, n), F32),
            vmem((4, 5, 24, n), F32),
            vmem((5, 24, n), BF16),
            vmem((5, 24, n), BF16),
            vmem((2, 5, 24, n), BF16),
            vmem((2, 5, 24, n), BF16),
            vmem((3, 8, 24, n), BF16),
        ]

    def body(*refs):
        kernel(own, items, *refs)

    inside = pl.BlockSpec(memory_space=pltpu.VMEM)
    outside = pl.BlockSpec(memory_space=pl.ANY)
    both = pl.pallas_call(
        body,
        out_shape=jax.ShapeDtypeStruct((24, width), BF16),
        in_specs=[inside] * 3 + [outside] * 3,
        out_specs=inside,
        scratch_shapes=scratch,
        compiler_params=pltpu.CompilerParams(
            collective_id=0, has_side_effects=True, vmem_limit_bytes=60 * 1024 * 1024
        ),
    )(section_input[0], saved_input[0], out_grad[0], gate_weight.swapaxes(1, 2),
      up_weight.swapaxes(1, 2), down_weight)
    return both[None, 0:12], both[None, 12:24]


def solution(mesh):
    spread = P("pipe", "tx", "ty")
    return jax.shard_map(
        local,
        mesh=mesh,
        in_specs=(spread, spread, spread, P("pipe", "ty", "tx"), P("pipe", "ty", "tx"), spread),
        out_specs=(spread, spread),
        check_vma=False,
    )
```

```python
import jax
import jax.numpy as jnp
from jax import lax
from jax.experimental import pallas as pl
from jax.experimental.pallas import tpu as pltpu
from jax.sharding import PartitionSpec as P

MESH = pl.DeviceIdType.MESH
F32 = jnp.float32
BF16 = jnp.bfloat16
CONTRACT_LAST = (((1,), (1,)), ((), ()))
N_SEM = 192
ORDER = (
    (0, 0), (0, 1), (0, 2), (1, 0), (0, 3), (1, 1), (1, 2), (2, 0),
    (7, 0), (1, 3), (2, 1), (2, 2), (0, 4), (3, 0), (2, 3), (0, 5),
    (3, 1), (3, 2), (1, 4), (4, 0), (0, 6), (3, 3), (1, 5), (4, 1),
    (0, 7), (4, 2), (1, 6), (2, 4), (5, 0), (4, 3), (1, 7), (2, 5),
    (6, 0), (5, 1), (5, 2), (2, 6), (6, 1), (3, 4), (6, 2), (5, 3),
    (2, 7), (3, 5), (6, 3), (3, 6), (4, 4), (3, 7), (4, 5), (4, 6),
    (5, 4), (4, 7), (5, 5), (6, 4), (5, 6), (6, 5), (5, 7), (6, 6),
    (6, 7),
)


def plan_of(total):
    own = -(-total // 32) * 16
    widths = [256] * (own // 256)
    widths.append(own - sum(widths))
    items = [(half, sum(widths[:i]), w) for half in range(2) for i, w in enumerate(widths)]
    return own, items


def kernel(own_units, items, si, sv, og, wg_hbm, wu_hbm, wd_hbm, both_out, *scratch):
    (wg, wu, wd, tmp, packs, xf, xb, acc_m, acc_b, pkf, ys, yr,
     z4s, z4r, zs, zr, fin, fin_r, wsem, ssem, rsem) = scratch[:21]
    per_chunk = [scratch[21 + 8 * c: 29 + 8 * c] for c in range(len(items))]

    pipe = lax.axis_index("pipe")
    tx = lax.axis_index("tx")
    ty = lax.axis_index("ty")
    ylo, z = tx // 8, tx % 8
    x, core = ty // 2, ty % 2
    partner = {"ty": x * 2 + (1 - core)}
    xp = {"ty": ((x + 1) % 4) * 2 + core}
    xm = {"ty": ((x + 3) % 4) * 2 + core}
    yp = {"tx": (1 - ylo) * 8 + z}
    zp = {"tx": ylo * 8 + (z + 1) % 8}
    zm = {"tx": ylo * 8 + (z + 7) % 8}
    across = {"pipe": 1 - pipe, "tx": (1 - ylo) * 8 + z}

    barrier = pltpu.get_barrier_semaphore()
    neighbours = (partner, xp, xm, yp, zp, zm, across)
    for neighbour in neighbours:
        pl.semaphore_signal(barrier, inc=1, device_id=neighbour, device_id_type=MESH)

    units = wd_hbm.shape[1]
    loads = [
        pltpu.make_async_copy(wg_hbm.at[0], wg.at[0:units], wsem.at[0]),
        pltpu.make_async_copy(wu_hbm.at[0], wu.at[0:units], wsem.at[1]),
        pltpu.make_async_copy(wd_hbm.at[0], wd.at[0:units], wsem.at[2]),
    ]
    for load in loads:
        load.start()
    for weight in (wg, wu, wd):
        weight[units:2 * own_units] = jnp.zeros((2 * own_units - units, weight.shape[1]), BF16)

    tmp[0:12] = si[...].astype(F32)
    tmp[12:24] = og[...].astype(F32)
    tmp[24:36] = sv[...].astype(F32)
    packs[0, 0] = tmp[...].astype(BF16)

    pl.semaphore_wait(barrier, len(neighbours))

    sent = []

    def send(src, dst, device):
        k = len(sent)
        copy = pltpu.make_async_remote_copy(
            src_ref=src, dst_ref=dst, send_sem=ssem.at[k], recv_sem=rsem.at[k],
            device_id=device, device_id_type=MESH,
        )
        copy.start()
        sent.append(copy)
        return copy

    def slab_of(zrel):
        return (zrel // 2 - x + 4) % 4

    def place(yrel, zrel):
        r = slab_of(zrel)
        lo = 12 * (zrel % 2)
        piece = packs[yrel, zrel].astype(F32)
        xf[0, yrel, r, lo:lo + 12] = piece[0:12]
        xf[1, yrel, r, lo:lo + 12] = piece[24:36]
        xf[2, yrel, r, lo:lo + 12] = piece[12:24]

    def operands(half):
        for a in range(3):
            xb[half, 96 * a:96 * a + 96] = xf[a, half].reshape(96, xf.shape[-1]).astype(BF16)

    lanes = packs.shape[-1] // 2

    def hop(source, target, device, before=None):
        copies = []
        for part in range(2):
            if before is not None:
                before[part].wait_recv()
            cols = slice(lanes * part, lanes * part + lanes)
            copies.append(send(packs.at[source[0], source[1], :, cols],
                               packs.at[target[0], target[1], :, cols], device))
        return copies

    def arrived(copies):
        for copy in copies:
            copy.wait_recv()

    y0, p1, m1 = [], [], []
    for part in range(2):
        cols = slice(lanes * part, lanes * part + lanes)
        mine = packs.at[0, 0, :, cols]
        p1.append(send(mine, packs.at[0, 7, :, cols], zp))
        m1.append(send(mine, packs.at[0, 1, :, cols], zm))
        y0.append(send(mine, packs.at[1, 0, :, cols], yp))
    place(0, 0)
    p2 = hop((0, 7), (0, 6), zp, p1)
    m2 = hop((0, 1), (0, 2), zm, m1)
    y7 = hop((0, 7), (1, 7), yp)
    y1 = hop((0, 1), (1, 1), yp)
    place(0, 7)
    place(0, 1)
    p3 = hop((0, 6), (0, 5), zp, p2)
    m3 = hop((0, 2), (0, 3), zm, m2)
    y6 = hop((0, 6), (1, 6), yp)
    y2 = hop((0, 2), (1, 2), yp)
    place(0, 6)
    place(0, 2)
    p4 = hop((0, 5), (0, 4), zp, p3)
    y5 = hop((0, 5), (1, 5), yp)
    y3 = hop((0, 3), (1, 3), yp, m3)
    place(0, 5)
    place(0, 3)
    y4 = hop((0, 4), (1, 4), yp, p4)
    place(0, 4)
    operands(0)
    for load in loads:
        load.wait()

    def second_half():
        for k, copies in ((0, y0), (7, y7), (1, y1), (6, y6), (2, y2), (5, y5), (3, y3), (4, y4)):
            arrived(copies)
            place(1, k)
        operands(1)

    state = [dict() for _ in items]

    def rows_of(c):
        half, offset, n = items[c]
        return [pl.ds(pl.multiple_of(who * own_units + offset, 16), n)
                for who in (core, 1 - core)]

    def compute(c):
        half, offset, n = items[c]
        own, sp, rp = per_chunk[c][:3]
        for target, rows in zip((own, sp), rows_of(c)):
            def keep(values, array):
                for r in range(4):
                    target[r, array] = values[24 * r:24 * r + 24]

            for first, weight in ((0, wg), (1, wu)):
                both = lax.dot_general(xb[half, 0:192], weight[rows, :], CONTRACT_LAST,
                                       preferred_element_type=F32)
                keep(both[0:96], first)
                keep(both[96:192], first + 2)
            keep(lax.dot_general(xb[half, 192:288], wd[rows, :], CONTRACT_LAST,
                                 preferred_element_type=F32), 4)
        state[c]["pair"] = send(sp.at[2:4], rp.at[2:4], partner)
        state[c]["pair2"] = send(sp.at[0:2], rp.at[0:2], partner)

    def stage_a(c):
        own, sp, rp, m1s, m1r = per_chunk[c][:5]
        na = 3 if c % 2 == 0 else 2
        state[c]["pair"].wait_recv()
        m1s[...] = (own[2] + rp[2]).astype(BF16)
        state[c]["m1p"] = send(m1s.at[0:na], m1r.at[0:na], xp)
        state[c]["m1m"] = send(m1s.at[na:5], m1r.at[na:5], xm)

    def stage_b(c):
        own, sp, rp, m1s, m1r, m2s, m2r = per_chunk[c][:7]
        na = 3 if c % 2 == 0 else 2
        state[c]["pair2"].wait_recv()
        state[c]["m1p"].wait_recv()
        for a in range(5):
            total = own[1, a] + rp[1, a]
            if a < na:
                total = total + m1r[a].astype(F32)
            m2s[0, a] = total.astype(BF16)
        state[c]["m2p"] = send(m2s.at[0], m2r.at[0], xp)
        state[c]["m1m"].wait_recv()
        for a in range(5):
            total = own[3, a] + rp[3, a]
            if a >= na:
                total = total + m1r[a].astype(F32)
            m2s[1, a] = total.astype(BF16)
        state[c]["m2m"] = send(m2s.at[1], m2r.at[1], xm)

    def stage_c(c):
        own, sp, rp, m1s, m1r, m2s, m2r, h = per_chunk[c][:8]
        state[c]["m2p"].wait_recv()
        state[c]["m2m"].wait_recv()
        gate, up, sgate, sup, hgrad = [
            own[0, a] + rp[0, a] + m2r[0, a].astype(F32) + m2r[1, a].astype(F32)
            for a in range(5)
        ]
        h[0, 0] = (gate * jax.nn.sigmoid(gate) * up).astype(BF16)
        q = jax.nn.sigmoid(sgate)
        h[1, 0] = (hgrad * sup * q * (1.0 + sgate * (1.0 - q))).astype(BF16)
        h[2, 0] = (hgrad * sgate * q).astype(BF16)
        state[c]["hp"] = send(h.at[:, 0], h.at[:, 3], xp)
        state[c]["hm"] = send(h.at[:, 0], h.at[:, 1], xm)
        state[c]["h0"] = send(h.at[:, 0], h.at[:, 4], partner)

    def stage_d(c):
        h = per_chunk[c][7]
        nb = 1 if c % 2 == 0 else 2
        state[c]["hp"].wait_recv()
        state[c]["hpp"] = send(h.at[0:nb, 3], h.at[0:nb, 2], xp)
        state[c]["hm"].wait_recv()
        state[c]["hmm"] = send(h.at[nb:3, 1], h.at[nb:3, 2], xm)
        state[c]["h3"] = send(h.at[:, 3], h.at[:, 7], partner)
        state[c]["h1"] = send(h.at[:, 1], h.at[:, 5], partner)

    def stage_e(c):
        h = per_chunk[c][7]
        state[c]["hpp"].wait_recv()
        state[c]["hmm"].wait_recv()
        state[c]["h2"] = send(h.at[:, 2], h.at[:, 6], partner)

    def stage_f(c):
        half, offset, n = items[c]
        h = per_chunk[c][7]
        for name in ("h0", "h1", "h3", "h2"):
            state[c][name].wait_recv()
        mixed, back = None, None
        for part, rows in enumerate(rows_of(c)):
            hidden, ggrad, ugrad = [
                h[a, 4 * part:4 * part + 4].astype(F32).reshape(96, n).astype(BF16)
                for a in range(3)
            ]
            one = jnp.dot(hidden, wd[rows, :], preferred_element_type=F32)
            two = jnp.dot(ggrad, wg[rows, :], preferred_element_type=F32)
            two = two + jnp.dot(ugrad, wu[rows, :], preferred_element_type=F32)
            mixed = one if mixed is None else mixed + one
            back = two if back is None else back + two
        mixed = mixed.reshape(4, 24, 1024)
        back = back.reshape(4, 24, 1024)
        if offset > 0:
            mixed = mixed + acc_m[half]
            back = back + acc_b[half]
        acc_m[half] = mixed
        acc_b[half] = back

    def packet(half, k):
        r = slab_of(k)
        lo = 12 * (k % 2)
        pkf[half, k, 0:12] = acc_m[half, r, lo:lo + 12]
        pkf[half, k, 12:24] = acc_b[half, r, lo:lo + 12]
        return pkf[half, k]

    ycopies = {}

    def first_sums():
        for k in (4, 3, 5, 2, 6, 1, 7, 0):
            ys[k] = packet(0, k).astype(BF16)
            ycopies[k] = send(ys.at[k], yr.at[k], yp)

    stages = (compute, stage_a, stage_b, stage_c, stage_d, stage_e, stage_f)
    count = len(items)
    for depth, c in ORDER:
        if depth == 7:
            second_half()
            continue
        stages[depth](c)
        if depth == 6 and c == count // 2 - 1:
            first_sums()

    def summed(k):
        ycopies[k].wait_recv()
        return packet(1, k) + yr[k].astype(F32)

    def cols_of(part):
        return slice(512 * part, 512 * part + 512)

    four = summed(4)
    links = ((0, zp, -1), (1, zm, 1))
    chain = {}
    for way, device, sign in links:
        z4s[way] = four[:, cols_of(way)].astype(BF16)
        chain[way, way] = send(z4s.at[way], z4r.at[way], device)
    for step in range(3):
        fresh = [summed(4 + sign * (step + 1)) for way, device, sign in links]
        for turn in range(2):
            for way, device, sign in links:
                part = 1 - way if turn == 0 else way
                cols = cols_of(part)
                value = fresh[way][:, cols]
                if step > 0 or part == way:
                    chain[way, part].wait_recv()
                    value = value + (z4r[way] if step == 0 else zr[way, step - 1, :, cols]).astype(F32)
                zs[way, step, :, cols] = value.astype(BF16)
                chain[way, part] = send(zs.at[way, step, :, cols], zr.at[way, step, :, cols], device)
    total = summed(0) + packs[1, 0].astype(F32)[0:24]
    last = []
    for part in range(2):
        cols = cols_of(part)
        value = total[:, cols]
        for way in range(2):
            chain[way, part].wait_recv()
            value = value + zr[way, 2, :, cols].astype(F32)
        fin[:, cols] = value.astype(BF16)
        last.append(send(fin.at[:, cols], fin_r.at[:, cols], across))
    arrived(last)
    both_out[...] = fin_r[...]
    for copy in sent:
        copy.wait_send()


def local(section_input, saved_input, out_grad, gate_weight, up_weight, down_weight):
    width, hidden = gate_weight.shape[1:]
    own, items = plan_of(hidden)
    rows = 2 * own
    vmem = pltpu.VMEM
    scratch = [
        vmem((rows, width), BF16),
        vmem((rows, width), BF16),
        vmem((rows, width), BF16),
        vmem((36, width), F32),
        vmem((2, 8, 36, width), BF16),
        vmem((3, 2, 4, 24, width), F32),
        vmem((2, 288, width), BF16),
        vmem((2, 4, 24, width), F32),
        vmem((2, 4, 24, width), F32),
        vmem((2, 8, 24, width), F32),
        vmem((8, 24, width), BF16),
        vmem((8, 24, width), BF16),
        vmem((2, 24, 512), BF16),
        vmem((2, 24, 512), BF16),
        vmem((2, 3, 24, width), BF16),
        vmem((2, 3, 24, width), BF16),
        vmem((24, width), BF16),
        vmem((24, width), BF16),
        pltpu.SemaphoreType.DMA((3,)),
        pltpu.SemaphoreType.DMA((N_SEM,)),
        pltpu.SemaphoreType.DMA((N_SEM,)),
    ]
    for _, _, n in items:
        scratch += [
            vmem((4, 5, 24, n), F32),
            vmem((4, 5, 24, n), F32),
            vmem((4, 5, 24, n), F32),
            vmem((5, 24, n), BF16),
            vmem((5, 24, n), BF16),
            vmem((2, 5, 24, n), BF16),
            vmem((2, 5, 24, n), BF16),
            vmem((3, 8, 24, n), BF16),
        ]

    def body(*refs):
        kernel(own, items, *refs)

    inside = pl.BlockSpec(memory_space=pltpu.VMEM)
    outside = pl.BlockSpec(memory_space=pl.ANY)
    both = pl.pallas_call(
        body,
        out_shape=jax.ShapeDtypeStruct((24, width), BF16),
        in_specs=[inside] * 3 + [outside] * 3,
        out_specs=inside,
        scratch_shapes=scratch,
        compiler_params=pltpu.CompilerParams(
            collective_id=0, has_side_effects=True, vmem_limit_bytes=60 * 1024 * 1024
        ),
    )(section_input[0], saved_input[0], out_grad[0], gate_weight.swapaxes(1, 2),
      up_weight.swapaxes(1, 2), down_weight)
    return both[None, 0:12], both[None, 12:24]


def solution(mesh):
    spread = P("pipe", "tx", "ty")
    return jax.shard_map(
        local,
        mesh=mesh,
        in_specs=(spread, spread, spread, P("pipe", "ty", "tx"), P("pipe", "ty", "tx"), spread),
        out_specs=(spread, spread),
        check_vma=False,
    )
```
